32 devices in a mesh: img: 8 (over z, core), feat: 4 (over y, x).
Axes of the slice: x: 2, y: 2, z: 4, core: 2. Of those that a mesh axis runs over, the one named last changes fastest.
Arguments:
- features: bfloat16 [8192, 32768], P('img', 'feat'), may hold values from -0.055242717 to 0.055242717
- weights: bfloat16 [512, 32768], P('img', 'feat'), may hold values from -20 to 20
- direction: bfloat16 [512, 32768], P('img', 'feat'), may hold values from -6 to 6
Outputs:
- hessian_product: float32 [512, 32768], P('img', 'feat')
The draws below stay inside these ranges and needn't reach their ends.
All inputs are finite; a program needn't handle non-finite values.
Results may differ from the reference program's by a relative error of at most 0.0024.
Values may be sent and summed in bfloat16 or wider, within the bound.
No kernel may reach another device: no remote copies, remote signals or barrier semaphores. Data moves between devices by JAX's collectives and lax.ppermute only.
A program may use at most 128 MiB of HBM per device.

```python
import jax
import jax.numpy as jnp
from jax import lax

FEATS = 32768
CLASSES = 512
ROWS_DEV = 1024
IMAGES = 8192


def draw_features(key, part):
    first = jax.random.fold_in(key, 11)
    base = jnp.clip(jax.random.normal(first, (IMAGES, FEATS), jnp.float32), -6.0, 6.0)
    return (jnp.clip(base, -10.0, 10.0) * FEATS ** (-0.5)).astype(jnp.bfloat16)


def draw_weights(key, part):
    first = jax.random.fold_in(key, 21)
    base = 2.0 * jnp.clip(jax.random.normal(first, (CLASSES, FEATS), jnp.float32), -6.0, 6.0)
    return jnp.clip(base, -20.0, 20.0).astype(jnp.bfloat16)


def block_levels(rng, extent, shards, smallest, top_value):
    loudness, own = 1.0, jax.random.fold_in(rng, 6)
    for position, blocks in shards:
        steps = jnp.exp(jax.random.uniform(jax.random.fold_in(own, position), (blocks,), jnp.float32, smallest / len(shards), top_value / len(shards)))
        loudness = loudness * jnp.repeat(steps, extent[position] // blocks).reshape([-1 if axis == position else 1 for axis in range(len(extent))])
    return loudness


def centred(rng, shape, width, most, shards=(), held_as=jnp.bfloat16):
    level = block_levels(rng, shape, shards, -0.22, 0.18) if shards else 1.0
    array = jax.random.normal(rng, shape, jnp.float32) * width * level
    return jnp.minimum(jnp.maximum(array, -most), most).astype(held_as)


def setup_inputs(seed: int = 0) -> dict:
    seeds = jax.random.split(jax.random.key(seed), 4)
    return {
        "features": draw_features(jax.random.fold_in(seeds[3], 71), 0),
        "weights": draw_weights(jax.random.fold_in(seeds[3], 71), 0),
        "direction": centred(seeds[2], (CLASSES, FEATS), 1.0, 6.0, ((0, 8), (1, 4))),
    }


def reference(features, weights, direction):
    wide_w = weights.astype(jnp.float32)
    wide_v = direction.astype(jnp.float32)
    blocks = features.reshape(IMAGES // ROWS_DEV, ROWS_DEV, FEATS)

    def step(total, block):
        rows = block.astype(jnp.float32)
        scores = jnp.dot(rows, wide_w.T, preferred_element_type=jnp.float32)
        slopes = jnp.dot(rows, wide_v.T, preferred_element_type=jnp.float32)
        prob = jax.nn.sigmoid(scores)
        curvature = (prob * (1.0 - prob) * slopes).astype(jnp.bfloat16).astype(jnp.float32)
        return total + jnp.dot(curvature.T, rows, preferred_element_type=jnp.float32), None

    total, unused = lax.scan(step, jnp.zeros((CLASSES, FEATS), jnp.float32), blocks)
    return 4.0 * total
```

```python
import functools

import jax
import jax.numpy as jnp
from jax import lax
from jax.experimental import pallas as pl
from jax.experimental.pallas import tpu as pltpu
from jax.sharding import PartitionSpec as P

MIB = 1024 * 1024
BF16, F32 = jnp.bfloat16, jnp.float32
VMEM = pl.BlockSpec(memory_space=pltpu.VMEM)
LIMIT = 28 * MIB


def over_lines(pairs):
    return [(2 * a + c, 2 * b + c) for a, b in pairs for c in range(2)]


def flipped(pairs):
    return [(b, a) for a, b in pairs]


def chunk_rows(rows):
    units = rows // 8
    count = min(units, 4)
    sizes = [units // count] * count
    for k in range(units - sum(sizes)):
        sizes[k] += 1
    while count > 1 and sizes[-1] > 1:
        sizes[-1] -= 1
        sizes[0] += 1
    return [8 * size for size in sizes]


def tiles(feats, block):
    return feats // block, lambda j: pl.ds(pl.multiple_of(j * block, block), block)


def forward_kernel(count, x_ref, *refs):
    pieces, (mine_ref, other_ref) = refs[:count], refs[count:]
    rows = mine_ref.shape[0]
    mine_ref[...] = jnp.zeros_like(mine_ref)
    other_ref[...] = jnp.zeros_like(other_ref)
    steps, at = tiles(x_ref.shape[1], min(2048, x_ref.shape[1]))

    @pl.loop(0, steps)
    def _(j):
        left = jnp.concatenate([piece[:, at(j)] for piece in pieces], axis=0)
        part = lax.dot_general(
            left, x_ref[:, at(j)], (((1,), (1,)), ((), ())), preferred_element_type=F32
        )
        mine_ref[...] += part[:rows]
        other_ref[...] += part[rows:]


def forward(x, mine, other):
    images, feats = x.shape
    pieces = mine + other
    rows = sum(piece.shape[0] for piece in mine)
    out = jax.ShapeDtypeStruct((rows, images), F32)
    return pl.pallas_call(
        functools.partial(forward_kernel, len(pieces)),
        in_specs=[VMEM] * (1 + len(pieces)),
        out_specs=[VMEM] * 2,
        out_shape=[out, out],
        compiler_params=pltpu.CompilerParams(vmem_limit_bytes=LIMIT),
        cost_estimate=pl.CostEstimate(
            flops=4 * rows * images * feats,
            bytes_accessed=2 * images * feats + 4 * rows * feats + 8 * rows * images,
            transcendentals=0,
        ),
        name="forward",
    )(x, *pieces)


def weigh(sums, rows):
    pairs = sums.reshape(-1, 2, rows, sums.shape[-1])
    prob = jax.nn.sigmoid(pairs[:, 0])
    return (prob * (1.0 - prob) * pairs[:, 1]).astype(BF16).reshape(-1, sums.shape[-1])


def backward_kernel(rows, x_ref, ta, ra, tb, rb, near_ref, far_ref, other_ref, curv):
    half, near = other_ref.shape[0], near_ref.shape[0]
    curv[:half] = weigh(ta[...] + ra[...], rows)
    curv[half:] = weigh(tb[...] + rb[...], rows)
    steps, at = tiles(x_ref.shape[1], min(1024, x_ref.shape[1]))

    @pl.loop(0, steps)
    def _(j):
        part = jnp.dot(curv[...], x_ref[:, at(j)], preferred_element_type=F32)
        near_ref[:, at(j)] = part[:near]
        far_ref[:, at(j)] = part[near:half]
        other_ref[:, at(j)] = part[half:]


def backward(x, ta, ra, tb, rb, rows):
    images, feats = x.shape
    half = ta.shape[0] // 2
    heights = (2 * rows, half - 2 * rows, half)
    return pl.pallas_call(
        functools.partial(backward_kernel, rows),
        in_specs=[VMEM] * 5,
        out_specs=[VMEM] * 3,
        out_shape=[jax.ShapeDtypeStruct((height, feats), F32) for height in heights],
        scratch_shapes=[pltpu.VMEM((2 * half, images), BF16)],
        compiler_params=pltpu.CompilerParams(vmem_limit_bytes=LIMIT),
        cost_estimate=pl.CostEstimate(
            flops=4 * half * images * feats,
            bytes_accessed=2 * images * feats + 32 * half * images + 8 * half * feats,
            transcendentals=2 * half * images,
        ),
        name="backward",
    )(x, ta, ra, tb, rb)


def body(lines, feat_devices, features, weights, direction):
    groups = lines // 2
    place = lax.axis_index("img") // 2
    even = place % 2 == 0
    swap_core = [(2 * a + c, 2 * a + 1 - c) for a in range(lines) for c in range(2)]
    swap_pair = over_lines([(a, a ^ 1) for a in range(lines)])
    bits = [1 << b for b in range(feat_devices.bit_length() - 1)]

    def edge(t):
        up = [(2 * q + 1, 2 * q + 2) for q in range(t - 1, groups - 1)]
        down = [(2 * q + 2, 2 * q + 1) for q in range(groups - t)]
        return over_lines(up + down)

    def inside(t):
        back = [(2 * q + 1, 2 * q) for q in range(groups - t)]
        onward = [(2 * q, 2 * q + 1) for q in range(t, groups)]
        return over_lines(back + onward)

    def across(value, bit):
        return lax.ppermute(value, "feat", [(f, f ^ bit) for f in range(feat_devices)])

    def img(value, pairs):
        return lax.ppermute(value, "img", pairs)

    def gathered(own):
        partner = img(own, swap_pair)
        pair = jnp.where(
            even,
            jnp.concatenate((own, partner), axis=0),
            jnp.concatenate((partner, own), axis=0),
        )
        first, second = {}, {0: pair}
        for t in range(1, groups):
            first[t] = img(second[t - 1], edge(t))
            second[t] = img(first[t], inside(t))
        slots = [pair]
        for m in range(1, groups):
            n = groups - m
            if m == n:
                slots.append(second[m] + first[m])
            else:
                slots.append(
                    jnp.where(even, second[m] + first[n], first[m] + second[n])
                )
        return slots, [img(slot, swap_core) for slot in slots]

    def reduced(ta, tb):
        for n, (a, b) in enumerate(zip(bits, reversed(bits))):
            ra, rb = across(ta, a), across(tb, b)
            if n == len(bits) - 1:
                return ta, ra, tb, rb
            ta, tb = ta + ra, tb + rb

    def summed(near, far, other, rows):
        got = img(other, swap_core)
        near = near + got[: 2 * rows]
        far = far + got[2 * rows :]
        slot = [None] + [far[2 * rows * m : 2 * rows * (m + 1)] for m in range(groups - 1)]
        carry = None
        for t in range(groups - 1, 0, -1):
            a, b = slot[t], slot[groups - t]
            if t != groups - t:
                a, b = jnp.where(even, a, b), jnp.where(even, b, a)
            if carry is not None:
                a = a + carry.astype(F32)
            got = img(a.astype(BF16), flipped(inside(t)))
            b = b + got.astype(F32)
            carry = img(b.astype(BF16), flipped(edge(t)))
        if carry is not None:
            near = near + carry.astype(F32)
        low, high = near[:rows], near[rows:]
        got = img(jnp.where(even, high, low).astype(BF16), swap_pair)
        return 4.0 * (jnp.where(even, low, high) + got.astype(F32))

    outs, start = [], 0
    for rows in chunk_rows(weights.shape[0]):
        take = slice(start, start + rows)
        own = jnp.concatenate((weights[take], direction[take]), axis=0)
        start += rows
        mine, other = gathered(own)
        sums = reduced(*forward(features, mine, other))
        outs.append(summed(*backward(features, *sums, rows), rows))
    return jnp.concatenate(outs, axis=0)


def solution(mesh):
    placed = (P("img", "feat"), P("img", "feat"), P("img", "feat"))
    return jax.shard_map(
        functools.partial(body, mesh.shape["img"] // 2, mesh.shape["feat"]),
        mesh=mesh,
        in_specs=placed,
        out_specs=P("img", "feat"),
        check_vma=False,
    )
```
